32 devices in a mesh: occ: 4 (over z), vir: 8 (over y, x, core).
Axes of the slice: x: 2, y: 2, z: 4, core: 2. Of those that a mesh axis runs over, the one named last changes fastest.
Arguments:
- amplitudes: bfloat16 [1280, 6144], P('occ', 'vir'), may hold values from -6 to 6
- ladder_tiles: bfloat16 [2304, 128, 128], P(('occ', 'vir')), may hold values from -0.078125 to 0.078125
- block_list: int32 [2304, 2], P(('occ', 'vir')), may hold values from -1 to 47, as said below
Outputs:
- residual: bfloat16 [1280, 6144], P('occ', 'vir')
The draws below stay inside these ranges and needn't reach their ends.
Inputs may be any that keep to these rules, and one draw needn't show every extreme that they name: `block_list`: rows come in runs of 72, one run a device, devices in the order occ then vir. A live row on vir index v has its out-tile among v's own tiles v * 6 to v * 6 + 5 and its in-tile among the 48 tiles of v's aligned group of 8 vir indices, both tiles of one irrep; each such equal-irrep pair stands once over the occ indices. Dead rows are -1, -1. Some vir index has all 72 rows live on every occ index.
All inputs are finite; a program needn't handle non-finite values.
Results may differ from the reference program's by a relative error of at most 0.001.
Values may be sent and summed in bfloat16 or wider, within the bound.
A program may use at most 64 MiB of HBM per device.

```python
import jax
import jax.numpy as jnp
from jax import lax

TV = 128
KT = 6
GROUP = 8
SQ = 72
NOCCP = 1280
NVP = 6144
NBLK = 2304
N_OCC = 4
N_VIR = 8


def draw_block_list(key, part):
    group_count = N_VIR // GROUP
    split_points = jax.random.randint(jax.random.fold_in(key, 11), (group_count,), 0, GROUP)
    forced = jax.random.randint(jax.random.fold_in(key, 12), (), 0, group_count)
    split_points = jnp.where(jnp.arange(group_count) == forced, 0, split_points)
    rank_keys = jax.random.split(jax.random.fold_in(key, 13), N_VIR)
    rank_perms = jax.vmap(lambda one_key: jax.random.permutation(one_key, SQ * N_OCC))(rank_keys).astype(jnp.int32)
    device_ids = jnp.arange(N_OCC * N_VIR, dtype=jnp.int32)
    occ_ids = device_ids // N_VIR
    vir_ids = device_ids % N_VIR
    group_ids = vir_ids // GROUP
    position = vir_ids % GROUP
    split_here = split_points[group_ids]
    in_lower = position < split_here
    first_device = jnp.where(in_lower, group_ids * GROUP, group_ids * GROUP + split_here)
    members = jnp.where(in_lower, split_here, GROUP - split_here)
    slot_ids = jnp.arange(SQ, dtype=jnp.int32)
    raw_rank = slot_ids[None, :] * N_OCC + occ_ids[:, None]
    block_rank = rank_perms[vir_ids[:, None], raw_rank]
    is_live = block_rank < KT * KT * members[:, None]
    out_tile = vir_ids[:, None] * KT + block_rank % KT
    in_tile = first_device[:, None] * KT + block_rank // KT
    out_tile = jnp.where(is_live, out_tile, -1)
    in_tile = jnp.where(is_live, in_tile, -1)
    return jnp.stack([in_tile, out_tile], axis=-1).reshape(N_OCC * N_VIR * SQ, 2).astype(jnp.int32)


def shard_levels(own_key, dims, cuts, smallest, largest):
    factor_of = 1.0
    for dim, parts in cuts:
        steps = jax.random.uniform(jax.random.fold_in(jax.random.fold_in(own_key, 6), dim), (parts,), jnp.float32, smallest / len(cuts), largest / len(cuts))
        factor_of = factor_of * jnp.repeat(jnp.exp(steps), dims[dim] // parts).reshape((-1,) + (1,) * (len(dims) - 1 - dim))
    return factor_of


def centred(stream_key, shape, deviation, most, cuts=(), kind=jnp.bfloat16):
    factor_of = shard_levels(stream_key, shape, cuts, -0.22, 0.18) if cuts else 1.0
    array = jax.random.normal(stream_key, shape, jnp.float32) * deviation * factor_of
    return jnp.minimum(jnp.maximum(array, -most), most).astype(kind)


def setup_inputs(seed: int = 0) -> dict:
    arg_keys = jax.random.split(jax.random.key(seed), 4)
    amplitudes = centred(arg_keys[0], (NOCCP, NVP), 1.0, 6.0, ((0, 4), (1, 8)))
    ladder_tiles = centred(arg_keys[1], (NBLK, TV, TV), (TV * KT * GROUP) ** -0.5, 0.078125, ((0, 32),))
    block_list = draw_block_list(jax.random.fold_in(arg_keys[3], 71), 0)
    return {"amplitudes": amplitudes, "ladder_tiles": ladder_tiles, "block_list": block_list}


def reference(amplitudes, ladder_tiles, block_list):
    tile_count = amplitudes.shape[1] // TV
    tiles_by_col = amplitudes.reshape(NOCCP, tile_count, TV)
    block_lists = block_list.reshape(N_OCC, N_VIR, SQ, 2)
    ladder_mats = ladder_tiles.reshape(N_OCC, N_VIR, SQ, TV, TV)

    def column(vir_index):
        entries = lax.dynamic_index_in_dim(block_lists, vir_index, 1, keepdims=False).reshape(N_OCC * SQ, 2)
        tile_mats = lax.dynamic_index_in_dim(ladder_mats, vir_index, 1, keepdims=False).reshape(N_OCC * SQ, TV, TV)
        in_tile = jnp.clip(entries[:, 0], 0, tile_count - 1).astype(jnp.int32)
        out_tile = entries[:, 1] - vir_index * KT
        picker = (out_tile[:, None] == jnp.arange(KT, dtype=jnp.int32)[None, :]).astype(jnp.float32)
        taken_cols = jnp.take(tiles_by_col, in_tile, axis=1).astype(jnp.float32)
        contrib = jnp.einsum("psk,skn->psn", taken_cols, tile_mats.astype(jnp.float32), precision=lax.Precision.HIGHEST)
        return jnp.einsum("psn,sa->pan", contrib, picker, precision=lax.Precision.HIGHEST)

    columns_out = lax.map(column, jnp.arange(N_VIR, dtype=jnp.int32))
    ladder = columns_out.transpose(1, 0, 2, 3).reshape(NOCCP, N_VIR * KT * TV)
    return ladder.astype(jnp.bfloat16)
```

```python
import jax
import jax.numpy as jnp
from jax import lax
from jax.experimental import pallas as pl
from jax.experimental.pallas import tpu as pltpu
from jax.sharding import PartitionSpec as P

TV = 128
GROUP = 8


def from_partner(block, axis, apart):
    count = lax.axis_size(axis)
    route = []
    for low in range(count):
        high = low | 1 << apart
        if high != low and high < count:
            route += [(low, high), (high, low)]
    return lax.ppermute(block, axis, route)


def collect_group(local_amps, vir_index):
    gathered = local_amps
    for bit_number in range(GROUP.bit_length() - 1):
        partner = from_partner(gathered, "vir", bit_number)
        is_low = vir_index >> bit_number & 1 == 0
        gathered = jnp.where(
            is_low,
            jnp.concatenate([gathered, partner], axis=1),
            jnp.concatenate([partner, gathered], axis=1),
        )
    return gathered


def ladder_block(group_amps, ladder_mats, block_pairs, vir_index, tiles_here):
    group_count = group_amps.shape[1] // TV
    first_tile = vir_index // GROUP * GROUP * tiles_here
    out_tile = block_pairs[:, 1] - vir_index * tiles_here
    in_tile = block_pairs[:, 0] - first_tile
    is_live = block_pairs[:, 1] >= 0
    pair_index = jnp.where(is_live, in_tile * tiles_here + out_tile, -1)
    slot_onehot = (
        pair_index[:, None] == jnp.arange(group_count * tiles_here, dtype=jnp.int32)[None, :]
    ).astype(jnp.bfloat16)
    placed = jnp.einsum(
        "sp,skn->pkn", slot_onehot, ladder_mats, preferred_element_type=jnp.float32
    ).astype(jnp.bfloat16)
    dense_weight = (
        placed.reshape(group_count, tiles_here, TV, TV)
        .transpose(0, 2, 1, 3)
        .reshape(group_count * TV, tiles_here * TV)
    )
    return jnp.dot(group_amps, dense_weight, preferred_element_type=jnp.float32)


def tiles_travel(amplitudes, ladder_tiles, block_list):
    tiles_here = amplitudes.shape[1] // TV
    vir_index = lax.axis_index("vir")
    all_tiles, all_pairs = (
        lax.all_gather(ladder_tiles, "occ", axis=0, tiled=True),
        lax.all_gather(block_list, "occ", axis=0, tiled=True),
    )
    group_amps = collect_group(amplitudes, vir_index)
    residual = ladder_block(group_amps, all_tiles, all_pairs, vir_index, tiles_here).astype(
        jnp.bfloat16
    )
    return residual


N_XY = 72
N_AMP = 12
N_PART = 10
N_SEM = N_XY + N_AMP + N_PART
FROM_PARTNER = {0: 0, 1: 1, 2: 2, 3: 3, 6: 4, 7: 5}
FROM_ACROSS = {0: 0, 4: 1, 5: 2, 7: 3}
HALF_OF = (0, 0, 0, 1, 0, 1, 1, 1)
CUT = 256


def find_slots(block_pairs, tiles_here):
    vir_index = lax.axis_index("vir")
    in_tile = block_pairs[:, 0] - vir_index // GROUP * GROUP * tiles_here
    out_tile = block_pairs[:, 1] - vir_index * tiles_here
    slots = block_pairs.shape[0]
    pair = jnp.where(block_pairs[:, 1] >= 0, in_tile * tiles_here + out_tile, -1)
    places = jnp.arange(GROUP * tiles_here * tiles_here, dtype=jnp.int32)
    hit = pair[:, None] == places[None, :]
    slot = jnp.arange(slots, dtype=jnp.int32)[:, None]
    return jnp.min(jnp.where(hit, slot, slots), axis=0)


def ladder_body(
    amps_hbm, tiles_hbm, slot_ref, out_ref, tiles_ref, dense_ref, all_ref, part, near, far,
    send_sems, recv_sems, load_sems
):
    o, v = lax.axis_index("occ"), lax.axis_index("vir")
    y, x, c = v // 4, v // 2 % 2, v % 2
    v_x = y * 4 + (1 - x) * 2 + c
    v_y = (1 - y) * 4 + x * 2 + c
    v_xy = (1 - y) * 4 + (1 - x) * 2 + c
    v_c = y * 4 + x * 2 + 1 - c
    upper = o // 2
    end, mid = 3 * upper, 1 + upper
    far_end, far_mid = 3 - end, 3 - mid
    is_end = o % 3 == 0
    is_mid = o % 3 != 0
    e = 1 - (o + 1) // 2 % 2
    partner = end + mid - o
    second = e * mid + (1 - e) * far_mid
    fifth = e * far_mid + (1 - e) * end
    block_of = (o, second, far_end, far_end, fifth, fifth, second, o)
    n_slots = tiles_hbm.shape[0]
    rows, width = out_ref.shape
    half, quarter = rows // 2, rows // 4
    whole = tuple(pl.ds(r * half, half) for r in range(2))
    top = tuple(pl.ds(r * half, quarter) for r in range(2))
    low = tuple(pl.ds(r * half + quarter, quarter) for r in range(2))

    load_amps = pltpu.make_async_copy(amps_hbm, all_ref.at[o, v], load_sems.at[0])
    load_amps.start()
    load_tiles = pltpu.make_async_copy(tiles_hbm, tiles_ref.at[pl.ds(0, n_slots)], load_sems.at[1])
    load_tiles.start()

    barrier = pltpu.get_barrier_semaphore()
    peers = [(partner, v), (o, v_x), (o, v_y), (o, v_c)]
    for peer in peers:
        pl.semaphore_signal(barrier, inc=1, device_id=peer, device_id_type=pl.DeviceIdType.MESH)

    @pl.when(is_mid)
    def _():
        pl.semaphore_signal(
            barrier, inc=1, device_id=(far_mid, v), device_id_type=pl.DeviceIdType.MESH
        )

    tiles_ref[n_slots] = jnp.zeros((TV, TV), tiles_ref.dtype)
    load_amps.wait()
    pl.semaphore_wait(barrier, len(peers) + 1 - e)

    def move(src, dst, number, peer):
        return pltpu.make_async_remote_copy(
            src_ref=src,
            dst_ref=dst,
            send_sem=send_sems.at[number],
            recv_sem=recv_sems.at[number],
            device_id=peer,
            device_id_type=pl.DeviceIdType.MESH,
        )

    def hop(block, tile, span, number, peer):
        ref = all_ref.at[block, tile, span]
        return move(ref, ref, number, peer)

    started = []

    def send(block, tile, span, number, peer):
        copy = hop(block, tile, span, number, peer)
        copy.start()
        started.append(copy)

    def arrived(block, tile, span, number, peer):
        hop(block, tile, span, number, peer).wait_recv()

    def own(k):
        block, r, base = block_of[k], HALF_OF[k], 9 * k
        send(block, v, whole[r], base, (o, v_x))
        send(block, v, whole[r], base + 1, (o, v_y))
        send(block, v, whole[r], base + 2, (o, v_c))

    def forward(k):
        block, r, base = block_of[k], HALF_OF[k], 9 * k
        arrived(block, v_x, whole[r], base, (o, v_x))
        send(block, v_x, top[r], base + 3, (o, v_y))
        send(block, v_x, whole[r], base + 4, (o, v_c))
        arrived(block, v_y, whole[r], base + 1, (o, v_y))
        send(block, v_y, low[r], base + 5, (o, v_x))
        send(block, v_y, whole[r], base + 6, (o, v_c))

    def corner(k):
        block, r, base = block_of[k], HALF_OF[k], 9 * k
        arrived(block, v_xy, top[r], base + 3, (o, v_y))
        send(block, v_xy, top[r], base + 7, (o, v_c))
        arrived(block, v_xy, low[r], base + 5, (o, v_x))
        send(block, v_xy, low[r], base + 8, (o, v_c))

    to_mid = [(end, 0), (end, 1)]
    to_end = [(mid, 0), (far_mid, 0), (far_end, 0), (far_end, 1), (far_mid, 1), (mid, 1)]
    to_far = [(mid, 0), (end, 0), (end, 1), (mid, 1)]
    from_far = [(far_mid, 0), (far_end, 0), (far_end, 1), (far_mid, 1)]

    def row_hop(chunk, number, peer):
        return hop(chunk[0], v, whole[chunk[1]], N_XY + number, (peer, v))

    def mid_sends(number):
        row_hop(to_end[number], 2 + number, end).start()

    def far_sends(number):
        row_hop(to_far[number], 8 + number, far_mid).start()

    def end_gets(number):
        @pl.when(is_end)
        def _():
            row_hop(to_end[number], 2 + number, mid).wait_recv()

    def product(k):
        block, r, base = block_of[k], HALF_OF[k], 9 * k
        o_v, o_x, o_y, o_xy = (t + 1 - 2 * c for t in (v, v_x, v_y, v_xy))
        arrived(block, o_v, whole[r], base + 2, (o, v_c))
        arrived(block, o_x, whole[r], base + 4, (o, v_c))
        arrived(block, o_y, whole[r], base + 6, (o, v_c))

        def add_up(tiles, first):
            for n in range(width // CUT):
                columns = pl.ds(n * CUT, CUT)
                total = None if first else part[k, :, columns]
                for tile in tiles:
                    depth = pl.ds(pl.multiple_of(tile * width, width), width)
                    term = jnp.dot(
                        all_ref[block, tile, whole[r]],
                        dense_ref[depth, columns],
                        preferred_element_type=jnp.float32,
                    )
                    total = term if total is None else total + term
                part[k, :, columns] = total

        add_up((v, v_x, v_y, o_v, o_x, o_y), True)
        arrived(block, o_xy, top[r], base + 7, (o, v_c))
        arrived(block, o_xy, low[r], base + 8, (o, v_c))
        add_up((v_xy, o_xy), False)

    def to_partner(k, slot):
        number = FROM_PARTNER[slot]
        return move(part.at[k], near.at[number], N_XY + N_AMP + number, (partner, v))

    def to_across(k, slot):
        number = FROM_ACROSS[slot]
        return move(part.at[k], far.at[number], N_XY + N_AMP + 6 + number, (far_mid, v))

    def end_posts(k, slot):
        @pl.when(is_end)
        def _():
            to_partner(k, slot).start()

    def mid_adds_near(k, slot):
        @pl.when(is_mid)
        def _():
            to_partner(k, k).wait_recv()
            part[k] += near[FROM_PARTNER[k]]
            to_across(k, slot).start()

    def mid_adds_far(k, slot):
        @pl.when(is_mid)
        def _():
            to_across(k, k).wait_recv()
            part[k] += far[FROM_ACROSS[k]]
            to_partner(k, slot).start()

    def finish(k):
        to_partner(k, k).wait_recv()

        @pl.when(is_end)
        def _():
            out_ref[whole[HALF_OF[k]], :] = (part[k] + near[FROM_PARTNER[k]]).astype(out_ref.dtype)

        @pl.when(is_mid)
        def _():
            to_across(k, k).wait_recv()
            out_ref[whole[HALF_OF[k]], :] = (
                part[k] + near[FROM_PARTNER[k]] + far[FROM_ACROSS[k]]
            ).astype(out_ref.dtype)

    @pl.when(is_end)
    def _():
        for number in range(2):
            row_hop(to_mid[number], number, mid).start()

    @pl.when(is_mid)
    def _():
        mid_sends(0)
        far_sends(0)

    own(0)

    load_tiles.wait()

    def place(k, carry):
        depth = pl.ds(pl.multiple_of(k * TV, TV), TV)
        for n in range(width // TV):
            dense_ref[depth, n * TV : (n + 1) * TV] = tiles_ref[slot_ref[k * (width // TV) + n]]
        return carry

    lax.fori_loop(0, dense_ref.shape[0] // TV, place, 0)

    @pl.when(is_mid)
    def _():
        row_hop(from_far[0], 8, far_mid).wait_recv()
        mid_sends(1)
        row_hop(to_mid[0], 0, end).wait_recv()
        far_sends(1)

    end_gets(0)
    own(1)
    forward(0)

    @pl.when(is_mid)
    def _():
        row_hop(from_far[1], 9, far_mid).wait_recv()
        mid_sends(2)
        row_hop(to_mid[1], 1, end).wait_recv()
        far_sends(2)
        far_sends(3)

    end_gets(2)
    own(2)
    forward(1)
    corner(0)

    @pl.when(is_mid)
    def _():
        row_hop(from_far[2], 10, far_mid).wait_recv()
        mid_sends(3)

    product(0)

    @pl.when(is_mid)
    def _():
        row_hop(from_far[3], 11, far_mid).wait_recv()
        mid_sends(4)
        mid_sends(5)

    end_gets(3)
    own(3)
    forward(2)
    corner(1)
    product(1)
    end_posts(1, 0)
    end_gets(1)
    own(4)
    forward(3)
    corner(2)
    product(2)
    end_posts(2, 2)
    end_gets(4)
    own(5)
    forward(4)
    corner(3)
    product(3)
    end_posts(3, 3)
    mid_adds_near(2, 4)
    end_gets(5)
    own(6)
    forward(5)
    corner(4)
    product(4)
    end_posts(4, 1)
    mid_adds_near(3, 5)
    own(7)
    forward(6)
    corner(5)
    product(5)
    end_posts(5, 6)
    mid_adds_far(4, 0)
    forward(7)
    corner(6)
    product(6)
    end_posts(6, 7)
    mid_adds_near(1, 0)
    mid_adds_near(6, 7)
    mid_adds_far(5, 7)
    corner(7)
    finish(0)
    product(7)
    finish(7)

    for copy in started:
        copy.wait_send()

    @pl.when(is_end)
    def _():
        for number in range(2):
            row_hop(to_mid[number], number, mid).wait_send()
        for k, slot in ((1, 0), (2, 2), (3, 3), (4, 1), (5, 6), (6, 7)):
            to_partner(k, slot).wait_send()

    @pl.when(is_mid)
    def _():
        for number in range(6):
            row_hop(to_end[number], 2 + number, end).wait_send()
        for number in range(4):
            row_hop(to_far[number], 8 + number, far_mid).wait_send()
        for k, slot in ((2, 4), (3, 5), (1, 0), (6, 7)):
            to_across(k, slot).wait_send()
        for k, slot in ((4, 0), (5, 7)):
            to_partner(k, slot).wait_send()


def tiles_stay(amplitudes, ladder_tiles, block_list):
    rows, width = amplitudes.shape
    n_occ, n_vir = lax.axis_size("occ"), lax.axis_size("vir")
    slots = ladder_tiles.shape[0]
    half = rows // 2
    return pl.pallas_call(
        ladder_body,
        out_shape=jax.ShapeDtypeStruct((rows, width), jnp.bfloat16),
        in_specs=[
            pl.BlockSpec(memory_space=pl.ANY),
            pl.BlockSpec(memory_space=pl.ANY),
            pl.BlockSpec(memory_space=pltpu.SMEM),
        ],
        out_specs=pl.BlockSpec(memory_space=pltpu.VMEM),
        scratch_shapes=[
            pltpu.VMEM((slots + 1, TV, TV), ladder_tiles.dtype),
            pltpu.VMEM((n_vir * width, width), ladder_tiles.dtype),
            pltpu.VMEM((n_occ, n_vir, rows, width), jnp.bfloat16),
            pltpu.VMEM((8, half, width), jnp.float32),
            pltpu.VMEM((len(FROM_PARTNER), half, width), jnp.float32),
            pltpu.VMEM((len(FROM_ACROSS), half, width), jnp.float32),
            pltpu.SemaphoreType.DMA((N_SEM,)),
            pltpu.SemaphoreType.DMA((N_SEM,)),
            pltpu.SemaphoreType.DMA((2,)),
        ],
        compiler_params=pltpu.CompilerParams(
            collective_id=0, has_side_effects=True, vmem_limit_bytes=48 << 20
        ),
        name="ladder",
    )(amplitudes, ladder_tiles, find_slots(block_list, width // TV))


def per_device(amplitudes, ladder_tiles, block_list):
    everywhere = lax.axis_size("occ") * amplitudes.size * GROUP * 2
    even = amplitudes.shape[0] % 64 == 0 and amplitudes.shape[1] % CUT == 0
    fits = everywhere <= 16 << 20 and even
    if lax.axis_size("vir") == GROUP and lax.axis_size("occ") == 4 and fits:
        return tiles_stay(amplitudes, ladder_tiles, block_list)
    return tiles_travel(amplitudes, ladder_tiles, block_list)


def solution(mesh):
    return jax.shard_map(
        per_device,
        mesh=mesh,
        in_specs=(P("occ", "vir"), P(("occ", "vir"), None, None), P(("occ", "vir"), None)),
        out_specs=P("occ", "vir"),
        check_vma=False,
    )
```

```python
import jax
import jax.numpy as jnp
from jax import lax
from jax.experimental import pallas as pl
from jax.experimental.pallas import tpu as pltpu
from jax.sharding import PartitionSpec as P

TV = 128
GROUP = 8


def from_partner(block, axis, apart):
    count = lax.axis_size(axis)
    route = []
    for low in range(count):
        high = low | 1 << apart
        if high != low and high < count:
            route += [(low, high), (high, low)]
    return lax.ppermute(block, axis, route)


def collect_group(local_amps, vir_index):
    gathered = local_amps
    for bit_number in range(GROUP.bit_length() - 1):
        partner = from_partner(gathered, "vir", bit_number)
        is_low = vir_index >> bit_number & 1 == 0
        gathered = jnp.where(
            is_low,
            jnp.concatenate([gathered, partner], axis=1),
            jnp.concatenate([partner, gathered], axis=1),
        )
    return gathered


def ladder_block(group_amps, ladder_mats, block_pairs, vir_index, tiles_here):
    group_count = group_amps.shape[1] // TV
    first_tile = vir_index // GROUP * GROUP * tiles_here
    out_tile = block_pairs[:, 1] - vir_index * tiles_here
    in_tile = block_pairs[:, 0] - first_tile
    is_live = block_pairs[:, 1] >= 0
    pair_index = jnp.where(is_live, in_tile * tiles_here + out_tile, -1)
    slot_onehot = (
        pair_index[:, None] == jnp.arange(group_count * tiles_here, dtype=jnp.int32)[None, :]
    ).astype(jnp.bfloat16)
    placed = jnp.einsum(
        "sp,skn->pkn", slot_onehot, ladder_mats, preferred_element_type=jnp.float32
    ).astype(jnp.bfloat16)
    dense_weight = (
        placed.reshape(group_count, tiles_here, TV, TV)
        .transpose(0, 2, 1, 3)
        .reshape(group_count * TV, tiles_here * TV)
    )
    return jnp.dot(group_amps, dense_weight, preferred_element_type=jnp.float32)


def tiles_travel(amplitudes, ladder_tiles, block_list):
    tiles_here = amplitudes.shape[1] // TV
    vir_index = lax.axis_index("vir")
    all_tiles, all_pairs = (
        lax.all_gather(ladder_tiles, "occ", axis=0, tiled=True),
        lax.all_gather(block_list, "occ", axis=0, tiled=True),
    )
    group_amps = collect_group(amplitudes, vir_index)
    residual = ladder_block(group_amps, all_tiles, all_pairs, vir_index, tiles_here).astype(
        jnp.bfloat16
    )
    return residual


N_XY = 72
N_AMP = 18
N_PART = 60
N_SEM = N_XY + N_AMP + N_PART
FROM_PARTNER = {0: 0, 1: 1, 2: 2, 3: 3, 6: 4, 7: 5}
FROM_ACROSS = {0: 0, 4: 1, 5: 2, 7: 3}
HALF_OF = (0, 0, 0, 1, 0, 1, 1, 1)
CUT = 256
FULL = 8388000.0


def find_slots(block_pairs, tiles_here):
    vir_index = lax.axis_index("vir")
    in_tile = block_pairs[:, 0] - vir_index // GROUP * GROUP * tiles_here
    out_tile = block_pairs[:, 1] - vir_index * tiles_here
    slots = block_pairs.shape[0]
    pair = jnp.where(block_pairs[:, 1] >= 0, in_tile * tiles_here + out_tile, -1)
    places = jnp.arange(GROUP * tiles_here * tiles_here, dtype=jnp.int32)
    hit = pair[:, None] == places[None, :]
    slot = jnp.arange(slots, dtype=jnp.int32)[:, None]
    return jnp.min(jnp.where(hit, slot, slots), axis=0)


def ladder_body(
    amps_hbm, tiles_hbm, slot_ref, out_ref, tiles_ref, dense_ref, all_ref, part, near, far,
    scale, near_scale, far_scale, code, send_sems, recv_sems, load_sems
):
    o, v = lax.axis_index("occ"), lax.axis_index("vir")
    y, x, c = v // 4, v // 2 % 2, v % 2
    v_x = y * 4 + (1 - x) * 2 + c
    v_y = (1 - y) * 4 + x * 2 + c
    v_xy = (1 - y) * 4 + (1 - x) * 2 + c
    v_c = y * 4 + x * 2 + 1 - c
    upper = o // 2
    end, mid = 3 * upper, 1 + upper
    far_end, far_mid = 3 - end, 3 - mid
    is_end = o % 3 == 0
    is_mid = o % 3 != 0
    e = 1 - (o + 1) // 2 % 2
    partner = end + mid - o
    second = e * mid + (1 - e) * far_mid
    fifth = e * far_mid + (1 - e) * end
    block_of = (o, second, far_end, far_end, fifth, fifth, second, o)
    n_slots = tiles_hbm.shape[0]
    rows, width = out_ref.shape
    half, quarter = rows // 2, rows // 4
    whole = tuple(pl.ds(r * half, half) for r in range(2))
    top = tuple(pl.ds(r * half, quarter) for r in range(2))
    low = tuple(pl.ds(r * half + quarter, quarter) for r in range(2))

    load_amps = pltpu.make_async_copy(amps_hbm, all_ref.at[o, v], load_sems.at[0])
    load_amps.start()
    load_tiles = pltpu.make_async_copy(tiles_hbm, tiles_ref.at[pl.ds(0, n_slots)], load_sems.at[1])
    load_tiles.start()

    barrier = pltpu.get_barrier_semaphore()
    peers = [(partner, v), (o, v_x), (o, v_y), (o, v_c)]
    for peer in peers:
        pl.semaphore_signal(barrier, inc=1, device_id=peer, device_id_type=pl.DeviceIdType.MESH)

    @pl.when(is_mid)
    def _():
        pl.semaphore_signal(
            barrier, inc=1, device_id=(far_mid, v), device_id_type=pl.DeviceIdType.MESH
        )

    tiles_ref[n_slots] = jnp.zeros((TV, TV), tiles_ref.dtype)
    load_amps.wait()
    pl.semaphore_wait(barrier, len(peers) + 1 - e)

    def move(src, dst, number, peer):
        return pltpu.make_async_remote_copy(
            src_ref=src,
            dst_ref=dst,
            send_sem=send_sems.at[number],
            recv_sem=recv_sems.at[number],
            device_id=peer,
            device_id_type=pl.DeviceIdType.MESH,
        )

    def hop(block, tile, span, number, peer):
        ref = all_ref.at[block, tile, span]
        return move(ref, ref, number, peer)

    started = []

    def send(block, tile, span, number, peer):
        copy = hop(block, tile, span, number, peer)
        copy.start()
        started.append(copy)

    def arrived(block, tile, span, number, peer):
        hop(block, tile, span, number, peer).wait_recv()

    def own(k):
        block, r, base = block_of[k], HALF_OF[k], 9 * k
        send(block, v, whole[r], base, (o, v_x))
        send(block, v, whole[r], base + 1, (o, v_y))
        send(block, v, whole[r], base + 2, (o, v_c))

    def forward(k):
        block, r, base = block_of[k], HALF_OF[k], 9 * k
        arrived(block, v_x, whole[r], base, (o, v_x))
        send(block, v_x, top[r], base + 3, (o, v_y))
        send(block, v_x, whole[r], base + 4, (o, v_c))
        arrived(block, v_y, whole[r], base + 1, (o, v_y))
        send(block, v_y, low[r], base + 5, (o, v_x))
        send(block, v_y, whole[r], base + 6, (o, v_c))

    def corner(k):
        block, r, base = block_of[k], HALF_OF[k], 9 * k
        arrived(block, v_xy, top[r], base + 3, (o, v_y))
        send(block, v_xy, top[r], base + 7, (o, v_c))
        arrived(block, v_xy, low[r], base + 5, (o, v_x))
        send(block, v_xy, low[r], base + 8, (o, v_c))

    spans = {"a": whole[0], "b": whole[1], "a0": top[0], "a1": low[0], "b0": top[1], "b1": low[1]}
    to_mid = [(end, "a0"), (end, "a1"), (end, "b0"), (end, "b1")]
    to_end = [
        (mid, "a"), (far_end, "a0"), (far_end, "a1"), (far_end, "b0"), (far_end, "b1"),
        (far_mid, "a"), (far_mid, "b"), (mid, "b"),
    ]
    to_far = [(mid, "a"), (end, "a0"), (end, "a1"), (end, "b0"), (end, "b1"), (mid, "b")]
    from_far = [
        (far_mid, "a"), (far_end, "a0"), (far_end, "a1"), (far_end, "b0"), (far_end, "b1"),
        (far_mid, "b"),
    ]

    def row_hop(chunk, number, peer):
        return hop(chunk[0], v, spans[chunk[1]], N_XY + number, (peer, v))

    def end_sends(number):
        row_hop(to_mid[number], number, mid).start()

    def mid_sends(number):
        row_hop(to_end[number], 4 + number, end).start()

    def far_sends(number):
        row_hop(to_far[number], 12 + number, far_mid).start()

    def end_gets(*numbers):
        @pl.when(is_end)
        def _():
            for number in numbers:
                row_hop(to_end[number], 4 + number, mid).wait_recv()

    def mid_gets(number):
        row_hop(to_mid[number], number, end).wait_recv()

    def far_gets(number):
        row_hop(from_far[number], 12 + number, far_mid).wait_recv()

    def product(k, then=None):
        block, r, base = block_of[k], HALF_OF[k], 9 * k
        o_v, o_x, o_y, o_xy = (t + 1 - 2 * c for t in (v, v_x, v_y, v_xy))
        arrived(block, o_v, whole[r], base + 2, (o, v_c))
        arrived(block, o_x, whole[r], base + 4, (o, v_c))
        arrived(block, o_y, whole[r], base + 6, (o, v_c))

        def add_up(tiles, first, then=None):
            for n in range(width // CUT):
                columns = pl.ds(n * CUT, CUT)
                total = None if first else part[k, n]
                for tile in tiles:
                    depth = pl.ds(pl.multiple_of(tile * width, width), width)
                    term = jnp.dot(
                        all_ref[block, tile, whole[r]],
                        dense_ref[depth, columns],
                        preferred_element_type=jnp.float32,
                    )
                    total = term if total is None else total + term
                part[k, n] = total
                if then is not None:
                    then(n)

        add_up((v, v_x, v_y, o_v, o_x, o_y), True)
        arrived(block, o_xy, top[r], base + 7, (o, v_c))
        arrived(block, o_xy, low[r], base + 8, (o, v_c))
        add_up((v_xy, o_xy), False, then)

    def encode(k, n):
        total = part[k, n]
        left, right = total[:, :TV], total[:, TV:]
        most = jnp.max(jnp.maximum(jnp.abs(left), jnp.abs(right)), axis=0, keepdims=True)
        most = jnp.maximum(most, 1e-30)
        scale[k, n] = jnp.broadcast_to(most * (1 / FULL), scale.shape[2:])
        grow = FULL / most
        left = jnp.round(left * grow).astype(jnp.int32)
        right = jnp.round(right * grow).astype(jnp.int32)
        code[k, n, :, :TV] = (left >> 8).astype(jnp.int16)
        code[k, n, :, TV:CUT] = (right >> 8).astype(jnp.int16)
        code[k, n, :, CUT:] = ((left & 255) + ((right & 255) << 8) - 32768).astype(jnp.int16)

    def decode(codes, scales):
        unit = scales[:1, :]
        tail = codes[:, CUT:].astype(jnp.int32) + 32768
        left = (codes[:, :TV].astype(jnp.int32) << 8) + (tail & 255)
        right = (codes[:, TV:CUT].astype(jnp.int32) << 8) + (tail >> 8)
        return jnp.concatenate(
            [left.astype(jnp.float32) * unit, right.astype(jnp.float32) * unit], axis=1
        )

    def to_partner(k, slot, n):
        number = FROM_PARTNER[slot]
        first = N_XY + N_AMP + 6 * number + 2 * n
        return (
            move(code.at[k, n], near.at[number, n], first, (partner, v)),
            move(scale.at[k, n], near_scale.at[number, n], first + 1, (partner, v)),
        )

    def to_across(k, slot, n):
        number = FROM_ACROSS[slot]
        first = N_XY + N_AMP + 36 + 6 * number + 2 * n
        return (
            move(code.at[k, n], far.at[number, n], first, (far_mid, v)),
            move(scale.at[k, n], far_scale.at[number, n], first + 1, (far_mid, v)),
        )

    def start(copies):
        for copy in copies:
            copy.start()

    def got_near(k, n):
        for copy in to_partner(k, k, n):
            copy.wait_recv()
        return decode(near[FROM_PARTNER[k], n], near_scale[FROM_PARTNER[k], n])

    def got_far(k, n):
        for copy in to_across(k, k, n):
            copy.wait_recv()
        return decode(far[FROM_ACROSS[k], n], far_scale[FROM_ACROSS[k], n])

    cuts = range(width // CUT)

    def end_posts(k, slot):
        def then(n):
            @pl.when(is_end)
            def _():
                encode(k, n)
                start(to_partner(k, slot, n))

        return then

    def mid_adds_near(k, slot):
        @pl.when(is_mid)
        def _():
            for n in cuts:
                part[k, n] += got_near(k, n)
                encode(k, n)
                start(to_across(k, slot, n))

    def mid_adds_far(k, slot):
        @pl.when(is_mid)
        def _():
            for n in cuts:
                part[k, n] += got_far(k, n)
                encode(k, n)
                start(to_partner(k, slot, n))

    def finish(k, n):
        part[k, n] += got_near(k, n)

        @pl.when(is_mid)
        def _():
            part[k, n] += got_far(k, n)

        out_ref[whole[HALF_OF[k]], pl.ds(n * CUT, CUT)] = part[k, n].astype(out_ref.dtype)

    @pl.when(is_end)
    def _():
        for number in range(4):
            end_sends(number)

    @pl.when(is_mid)
    def _():
        mid_sends(0)
        far_sends(0)

    own(0)

    load_tiles.wait()

    def place(k, carry):
        depth = pl.ds(pl.multiple_of(k * TV, TV), TV)
        for n in range(width // TV):
            dense_ref[depth, n * TV : (n + 1) * TV] = tiles_ref[slot_ref[k * (width // TV) + n]]
        return carry

    lax.fori_loop(0, dense_ref.shape[0] // TV, place, 0)

    @pl.when(is_mid)
    def _():
        mid_gets(0)
        far_sends(1)
        mid_gets(1)
        far_sends(2)
        far_gets(0)

    end_gets(0)
    own(1)
    forward(0)

    @pl.when(is_mid)
    def _():
        far_gets(1)
        mid_sends(1)
        mid_gets(2)
        far_sends(3)
        far_gets(2)
        mid_sends(2)
        mid_gets(3)
        far_sends(4)
        far_sends(5)

    end_gets(1, 2)
    own(2)

    @pl.when(is_mid)
    def _():
        far_gets(3)
        mid_sends(3)

    forward(1)
    corner(0)

    @pl.when(is_mid)
    def _():
        far_gets(4)
        mid_sends(4)
        mid_sends(5)

    product(0)
    end_gets(3, 4)
    own(3)
    forward(2)
    corner(1)

    @pl.when(is_mid)
    def _():
        far_gets(5)
        mid_sends(6)
        mid_sends(7)

    product(1, end_posts(1, 0))
    end_gets(5)
    own(4)
    forward(3)
    corner(2)
    product(2, end_posts(2, 2))
    end_gets(6)
    own(5)
    mid_adds_near(2, 4)
    forward(4)
    corner(3)
    product(3, end_posts(3, 3))
    end_gets(7)
    own(6)
    mid_adds_near(3, 5)
    forward(5)
    corner(4)
    product(4, end_posts(4, 1))
    own(7)
    mid_adds_far(4, 0)
    mid_adds_near(1, 0)
    forward(6)
    corner(5)
    product(5, end_posts(5, 6))
    mid_adds_far(5, 7)
    forward(7)
    corner(6)
    product(6, end_posts(6, 7))
    mid_adds_near(6, 7)
    corner(7)
    for n in cuts:
        finish(0, n)
    product(7)
    for n in cuts:
        finish(7, n)

    for copy in started:
        copy.wait_send()

    def sent(way, k, slot):
        for n in cuts:
            for copy in way(k, slot, n):
                copy.wait_send()

    @pl.when(is_end)
    def _():
        for number in range(4):
            row_hop(to_mid[number], number, mid).wait_send()
        for k, slot in ((1, 0), (2, 2), (3, 3), (4, 1), (5, 6), (6, 7)):
            sent(to_partner, k, slot)

    @pl.when(is_mid)
    def _():
        for number in range(8):
            row_hop(to_end[number], 4 + number, end).wait_send()
        for number in range(6):
            row_hop(to_far[number], 12 + number, far_mid).wait_send()
        for k, slot in ((2, 4), (3, 5), (1, 0), (6, 7)):
            sent(to_across, k, slot)
        for k, slot in ((4, 0), (5, 7)):
            sent(to_partner, k, slot)


def tiles_stay(amplitudes, ladder_tiles, block_list):
    rows, width = amplitudes.shape
    n_occ, n_vir = lax.axis_size("occ"), lax.axis_size("vir")
    slots = ladder_tiles.shape[0]
    half, cuts = rows // 2, width // CUT
    return pl.pallas_call(
        ladder_body,
        out_shape=jax.ShapeDtypeStruct((rows, width), jnp.bfloat16),
        in_specs=[
            pl.BlockSpec(memory_space=pl.ANY),
            pl.BlockSpec(memory_space=pl.ANY),
            pl.BlockSpec(memory_space=pltpu.SMEM),
        ],
        out_specs=pl.BlockSpec(memory_space=pltpu.VMEM),
        scratch_shapes=[
            pltpu.VMEM((slots + 1, TV, TV), ladder_tiles.dtype),
            pltpu.VMEM((n_vir * width, width), ladder_tiles.dtype),
            pltpu.VMEM((n_occ, n_vir, rows, width), jnp.bfloat16),
            pltpu.VMEM((8, cuts, half, CUT), jnp.float32),
            pltpu.VMEM((len(FROM_PARTNER), cuts, half, CUT + TV), jnp.int16),
            pltpu.VMEM((len(FROM_ACROSS), cuts, half, CUT + TV), jnp.int16),
            pltpu.VMEM((8, cuts, 8, TV), jnp.float32),
            pltpu.VMEM((len(FROM_PARTNER), cuts, 8, TV), jnp.float32),
            pltpu.VMEM((len(FROM_ACROSS), cuts, 8, TV), jnp.float32),
            pltpu.VMEM((8, cuts, half, CUT + TV), jnp.int16),
            pltpu.SemaphoreType.DMA((N_SEM,)),
            pltpu.SemaphoreType.DMA((N_SEM,)),
            pltpu.SemaphoreType.DMA((2,)),
        ],
        compiler_params=pltpu.CompilerParams(
            collective_id=0, has_side_effects=True, vmem_limit_bytes=59 << 20
        ),
        name="ladder",
    )(amplitudes, ladder_tiles, find_slots(block_list, width // TV))


def per_device(amplitudes, ladder_tiles, block_list):
    everywhere = lax.axis_size("occ") * amplitudes.size * GROUP * 2
    even = amplitudes.shape[0] % 64 == 0 and amplitudes.shape[1] % CUT == 0
    fits = everywhere <= 16 << 20 and even
    if lax.axis_size("vir") == GROUP and lax.axis_size("occ") == 4 and fits:
        return tiles_stay(amplitudes, ladder_tiles, block_list)
    return tiles_travel(amplitudes, ladder_tiles, block_list)


def solution(mesh):
    return jax.shard_map(
        per_device,
        mesh=mesh,
        in_specs=(P("occ", "vir"), P(("occ", "vir"), None, None), P(("occ", "vir"), None)),
        out_specs=P("occ", "vir"),
        check_vma=False,
    )
```
